512 devices in a mesh: row: 32 (over x, z_lo, core), col: 16 (over z_hi, y).
Axes of the slice: x: 4, y: 4, z: 16 (z_hi: 4, z_lo: 4; z = z_hi * 4 + z_lo), core: 2. Of those that a mesh axis runs over, the one named last changes fastest.
Arguments:
- laplacian: bfloat16 [32768, 32768], P('row', 'col')
- interp: bfloat16 [32768, 128], P('row'), may hold values from -0.375 to 0.375
- vectors: bfloat16 [32, 32768], P(None, 'row'), may hold values from -6 to 6
- pairs: int32 [128, 2], replicated, may hold values from 0 to 255, as said below
Outputs:
- coarse: bfloat16 [16384, 16384], P(('row', 'col'))
- coarse_vectors: bfloat16 [32, 16384], P(None, 'row')
The draws below stay inside these ranges and needn't reach their ends.
Inputs may be any that keep to these rules, and one draw needn't show every extreme that they name: Row c holds (a, b), where a lies among the 8 fine tile rows of row index g = (c // 4) mod 16, that is a // 8 == g, and b // 8 == g + 16. Every fine tile row appears exactly once in pairs.
All inputs are finite; a program needn't handle non-finite values.
Results may differ from the reference program's by a relative error of at most 0.0058.
Values may be sent and summed in bfloat16 or wider, within the bound.
A program may use at most 64 MiB of HBM per device.

```python
import jax
import jax.numpy as jnp
from jax import lax

B = 128
K = 32
TR = 8
NT = 256
NV = 32768
NC = 128
GROUPS = 16


def draw_laplacian(key, part):
    vertex_count = NT * B
    first_key = jax.random.fold_in(key, 0)
    base_draw = jax.random.normal(first_key, (vertex_count, vertex_count), jnp.float32)
    symmetric = (base_draw + base_draw.T) * 0.7071
    identity = jnp.eye(vertex_count, dtype=jnp.float32)
    return (symmetric + 3.0 * identity).astype(jnp.bfloat16)


def draw_pairs(key, part):
    half_rows = TR // 2
    all_keys = jax.random.split(key, 2 * GROUPS)
    matching = jax.vmap(lambda sub_key: jax.random.permutation(sub_key, TR))(all_keys[:GROUPS]).astype(jnp.int32)
    ordering = jax.vmap(lambda sub_key: jax.random.permutation(sub_key, TR))(all_keys[GROUPS:]).astype(jnp.int32)
    group_ids = jnp.arange(GROUPS, dtype=jnp.int32)[:, None]
    low_rows = group_ids * TR + ordering
    high_rows = (group_ids + GROUPS) * TR + jnp.take_along_axis(matching, ordering, axis=1)
    stacked = jnp.stack([low_rows, high_rows], axis=-1)
    front_half = stacked[:, :half_rows].reshape(GROUPS * half_rows, 2)
    back_half = stacked[:, half_rows:].reshape(GROUPS * half_rows, 2)
    return jnp.concatenate([front_half, back_half], axis=0).astype(jnp.int32)


def steps_of(own_key, extent, shards, low, high):
    level = 1.0
    for position, shards_of in shards:
        draws = jax.random.uniform(jax.random.fold_in(jax.random.fold_in(own_key, 6), position), (shards_of,), jnp.float32, low / len(shards), high / len(shards))
        level = level * jnp.repeat(jnp.exp(draws), extent[position] // shards_of).reshape((-1,) + (1,) * (len(extent) - 1 - position))
    return level


def gaussian(rng, dims, width, reach, pieces=(), kind=jnp.bfloat16):
    values = jax.random.normal(rng, dims, jnp.float32) * width
    if len(pieces) > 0:
        values = steps_of(rng, dims, pieces, -0.22, 0.18) * values
    return jnp.clip(values, min=-reach, max=reach).astype(kind)


def setup_inputs(seed: int = 0) -> dict:
    key_of = jax.random.split(jax.random.key(seed), 5)
    laplacian = draw_laplacian(jax.random.fold_in(key_of[4], 71), 0)
    interp = gaussian(key_of[1], (NV, B), (2 * B) ** -0.5, 0.375, ((0, 32),))
    vectors = gaussian(key_of[2], (K, NV), 1.0, 6.0, ((1, 32),))
    pairs = draw_pairs(jax.random.fold_in(key_of[4], 71), 0)
    return {"laplacian": laplacian, "interp": interp, "vectors": vectors, "pairs": pairs}


def reference(laplacian, interp, vectors, pairs):
    fine_tiles = laplacian.reshape(NT, B, NT, B)
    interp_blocks = interp.reshape(NT, B, B).astype(jnp.float32)

    def project_row(operands):
        row_tiles, left_block = operands
        product = jnp.einsum('xjy,jyb->xjb', row_tiles.astype(jnp.float32), interp_blocks).astype(jnp.bfloat16)
        return jnp.einsum('xa,xjb->ajb', left_block, product.astype(jnp.float32)).astype(jnp.bfloat16)

    projected = lax.map(project_row, (fine_tiles, interp_blocks))
    low_member = pairs[:, 0].astype(jnp.int32)
    high_member = pairs[:, 1].astype(jnp.int32)
    row_sum = jnp.take(projected, low_member, axis=0).astype(jnp.float32) + jnp.take(projected, high_member, axis=0).astype(jnp.float32)
    coarse = jnp.take(row_sum, low_member, axis=2) + jnp.take(row_sum, high_member, axis=2)
    coarse = coarse.astype(jnp.bfloat16).reshape(NC * B, NC * B)
    restricted = jnp.einsum('kix,ixa->kia', vectors.reshape(K, NT, B).astype(jnp.float32), interp_blocks).astype(jnp.bfloat16)
    coarse_vectors = jnp.take(restricted, low_member, axis=1).astype(jnp.float32) + jnp.take(restricted, high_member, axis=1).astype(jnp.float32)
    coarse_vectors = coarse_vectors.astype(jnp.bfloat16).reshape(K, NC * B)
    return coarse, coarse_vectors
```

```python
import jax
import jax.numpy as jnp
from jax import lax
from jax.experimental import pallas as pl
from jax.experimental.pallas import tpu as pltpu
from jax.sharding import PartitionSpec as P

MESH = pl.DeviceIdType.MESH
F32 = jnp.float32
BF16 = jnp.bfloat16

TILE = 128
ROWS = 32
COLS = 16
FINE_ROWS = 8
FINE_COLS = 16
KEEP = 4
STEPS = 16
AHEAD = 6
FIRST = 1
WIDE = 4 * TILE
STRIP = 32
COARSE = 16384
PIECES = 4
HALF = PIECES // 2
PIECE = FINE_ROWS * TILE // PIECES


def prepare(
    pairs, lap_hbm, interp_hbm, vec_hbm, give_hbm, keep_hbm, block_hbm, vgive, vkeep,
    lap, own, vec, give, keep, block, in_sem, out_sem,
):
    row = lax.axis_index("row")
    col = lax.axis_index("col")
    partner = (row + ROWS // 2) % ROWS
    upper = row // (ROWS // 2)
    right = col // (COLS // 2)
    span = col % (COLS // 2)

    def wanted(k):
        return pairs[upper, KEEP * partner + k] - FINE_ROWS * row

    def kept(k):
        return pairs[upper, KEEP * row + k] - FINE_ROWS * row

    def tile_at(i):
        return pl.ds(pl.multiple_of(i * TILE, TILE), TILE)

    own_in = pltpu.make_async_copy(interp_hbm, own, in_sem.at[8])
    own_in.start()
    members = [wanted(k) for k in range(KEEP)] + [kept(k) for k in range(KEEP)]
    lap_in = []
    for n, i in enumerate(members):
        lap_in.append(pltpu.make_async_copy(lap_hbm.at[tile_at(i)], lap.at[n], in_sem.at[n]))
        lap_in[-1].start()
    vec_in = pltpu.make_async_copy(vec_hbm, vec, in_sem.at[9])
    vec_in.start()
    own_in.wait()

    for u in range(FINE_ROWS):
        d = (u // 4) * 64 + 4 * (row % (ROWS // 2)) + u % 4
        block[u * TILE : (u + 1) * TILE, :] = own[tile_at(pairs[upper, d] - FINE_ROWS * row), :]
    out = [pltpu.make_async_copy(block, block_hbm, out_sem.at[8])]
    out[0].start()

    vec_in.wait()
    for n, i in enumerate(members):
        part = jnp.dot(vec[:, tile_at(i)], own[tile_at(i), :], preferred_element_type=F32).astype(BF16)
        k = n % KEEP
        (vgive if n < KEEP else vkeep)[:, k * TILE : (k + 1) * TILE] = part

    across = [
        tile_at(pairs[right, (q % 2) * 64 + 8 * span + (q // 2) * 4 + v] - FINE_COLS * col)
        for q in range(4)
        for v in range(4)
    ]
    for n, i in enumerate(members):
        lap_in[n].wait()
        k = n % KEEP
        mine = own[tile_at(i), :]
        for q in range(4):
            wide = jnp.concatenate([lap[n, :, across[4 * q + v]] for v in range(4)], axis=1)
            part = lax.dot_general(mine, wide, (((0,), (0,)), ((), ())), preferred_element_type=F32)
            if n < KEEP:
                give[k, q] = part.astype(BF16)
            else:
                keep[k, q] = part
        src, dst = (give, give_hbm) if n < KEEP else (keep, keep_hbm)
        out.append(pltpu.make_async_copy(src.at[k], dst.at[k], out_sem.at[n]))
        out[-1].start()
    for copy in out:
        copy.wait()


def kernel(
    give, keep_hbm, block_hbm, vgive, vkeep, strips, cvec,
    keep, cols, trecv, rsend, vrecv,
    in_sem, xs_sem, xr_sem, zs_sem, zr_sem, ps_sem, pr_sem, v_sem, z_word, y_word,
):
    row = lax.axis_index("row")
    col = lax.axis_index("col")
    x, zlo, core = row // 8, (row // 2) % 4, row % 2
    zhi, y = col // 4, col % 4
    partner = (row + ROWS // 2) % ROWS
    x_up, x_down = (row + 8) % ROWS, (row + 24) % ROWS
    z_up, z_down = row + 2, row - 2
    twin = row + 1 - 2 * core

    barrier = pltpu.get_barrier_semaphore()

    def greet(r, c):
        pl.semaphore_signal(barrier, inc=1, device_id=(r, c), device_id_type=MESH)

    greet(partner, col)
    greet(x_up, col)
    greet(x_down, col)
    greet(twin, col)

    @pl.when(zlo < 3)
    def _():
        greet(z_up, col)

    @pl.when(zlo > 0)
    def _():
        greet(z_down, col)

    z_mates = [(zhi + 1) % 4 * 4 + y, (zhi + 3) % 4 * 4 + y]
    y_mates = [zhi * 4 + (y + o) % 4 for o in range(1, 4)]
    for c in z_mates + y_mates:
        greet(row, c)

    on_row = zlo == y
    dx = (x - zhi + 4) % 4
    is_source = jnp.logical_and(on_row, dx == 0)
    relay = jnp.logical_not(is_source)
    lead = core == 0
    follow = jnp.logical_not(lead)
    mine = pl.ds(pl.multiple_of(core * FINE_ROWS * TILE, FINE_ROWS * TILE), FINE_ROWS * TILE)

    @pl.when(is_source)
    def _():
        copy = pltpu.make_async_copy(block_hbm, cols.at[mine], in_sem.at[1])
        copy.start()
        copy.wait()

    keep_in = pltpu.make_async_copy(keep_hbm, keep, in_sem.at[0])
    keep_in.start()

    greeted = 9 + jnp.where(zlo < 3, 1, 0) + jnp.where(zlo > 0, 1, 0)
    pl.semaphore_wait(barrier, greeted)

    def piece_copy(p, f, target, sem):
        part = cols.at[pl.ds(pl.multiple_of(core * FINE_ROWS * TILE + p * PIECE, PIECE), PIECE)]
        return pltpu.make_async_remote_copy(
            src_ref=part, dst_ref=part, send_sem=ps_sem.at[p * 5 + f], recv_sem=pr_sem.at[sem],
            device_id=(target, col), device_id_type=MESH,
        )

    def forwards(p):
        first = dx == 1 if p % 2 == 0 else dx == 9
        second = dx == 3 if p % 2 == 1 else dx == 9
        return [
            (jnp.logical_and(on_row, jnp.logical_or(dx == 0, first)), piece_copy(p, 0, x_up, p)),
            (jnp.logical_and(on_row, jnp.logical_or(dx == 0, second)), piece_copy(p, 1, x_down, p)),
            (jnp.logical_and(zlo >= y, zlo < 3), piece_copy(p, 2, z_up, p)),
            (jnp.logical_and(zlo <= y, zlo > 0), piece_copy(p, 3, z_down, p)),
            (None, piece_copy(p, 4, twin, PIECES + p)),
        ]

    def when(test, act):
        if test is None:
            act()
        else:
            pl.when(test)(act)

    def pass_on(p):
        for test, copy in forwards(p):
            when(test, copy.start)

    def set_out():
        for p in range(PIECES):
            pass_on(p)

    def take_pieces():
        for p in range(PIECES):
            piece_copy(p, 0, twin, p).wait_recv()
            pass_on(p)

    def twin_half(n):
        for p in range(n * HALF, (n + 1) * HALF):
            other = cols.at[pl.ds(pl.multiple_of((1 - core) * FINE_ROWS * TILE + p * PIECE, PIECE), PIECE)]
            pltpu.make_async_remote_copy(
                src_ref=other, dst_ref=other, send_sem=ps_sem.at[p * 5 + 4], recv_sem=pr_sem.at[PIECES + p],
                device_id=(twin, col), device_id_type=MESH,
            ).wait_recv()

    def part_of(t):
        far = t < 12
        q = jnp.where(far, t // 3, t - 12)
        k = jnp.where(far, (zhi + t % 3 + 1) % 4, zhi)
        return k, q

    def x_copy(t):
        k, q = part_of(t)
        return pltpu.make_async_remote_copy(
            src_ref=give.at[k, q], dst_ref=trecv.at[t], send_sem=xs_sem.at[t], recv_sem=xr_sem.at[t],
            device_id=(partner, col), device_id_type=MESH,
        )

    pl.when(jnp.logical_and(lead, is_source))(set_out)
    for t in range(FIRST):
        x_copy(t).start()
    for c in z_mates:
        pl.semaphore_signal(z_word, inc=1, device_id=(row, c), device_id_type=MESH)
    pl.when(jnp.logical_and(lead, relay))(take_pieces)
    pl.semaphore_wait(z_word, 2)
    for c in y_mates:
        pl.semaphore_signal(y_word, inc=1, device_id=(row, c), device_id_type=MESH)
    pl.when(jnp.logical_and(follow, is_source))(set_out)
    pl.when(jnp.logical_and(follow, relay))(take_pieces)
    for t in range(FIRST, AHEAD):
        x_copy(t).start()
    v_copy = pltpu.make_async_remote_copy(
        src_ref=vgive, dst_ref=vrecv, send_sem=v_sem.at[0], recv_sem=v_sem.at[1],
        device_id=(partner, col), device_id_type=MESH,
    )
    v_copy.start()
    keep_in.wait()
    pl.semaphore_wait(y_word, 3)

    def window(c, q):
        start = (q % 2) * (COARSE // 2) + (2 * (c % 8) + q // 2) * WIDE
        return strips.at[c // 8, :, pl.ds(pl.multiple_of(start, WIDE), WIDE)]

    def quarter(t, at):
        return rsend.at[t, pl.ds(pl.multiple_of(at * STRIP, STRIP), STRIP)]

    def z_copy(t, o):
        k, q = part_of(t)
        at = (y + o) % 4
        return pltpu.make_async_remote_copy(
            src_ref=quarter(t, at), dst_ref=window(col, q), send_sem=zs_sem.at[t * 4 + o],
            recv_sem=zr_sem.at[col * 4 + q], device_id=(row, k * 4 + at), device_id_type=MESH,
        )

    def stay_copy(t):
        q = t - 12
        return pltpu.make_async_copy(quarter(t, y), window(col, q), zr_sem.at[col * 4 + q])

    def finish(t):
        @pl.when(t + AHEAD < STEPS)
        def _():
            x_copy(t + AHEAD).start()

        x_copy(t).wait_recv()
        k, q = part_of(t)
        total = (keep[k, q] + trecv[t].astype(F32)).astype(BF16)
        for v in range(4):
            here = slice(v * TILE, (v + 1) * TILE)
            there = pl.ds(pl.multiple_of((q * 4 + v) * TILE, TILE), TILE)
            rsend[t, :, here] = jnp.dot(
                total[:, here], cols[there, :], preferred_element_type=F32
            ).astype(BF16)

    def away(t, _):
        finish(t)
        for o in range(4):
            z_copy(t, o).start()
        return 0

    def near(t, _):
        finish(t)
        for o in range(1, 4):
            z_copy(t, o).start()
        stay_copy(t).start()
        return 0

    pl.when(follow)(lambda: twin_half(0))
    lax.fori_loop(0, 3, away, 0)
    pl.when(follow)(lambda: twin_half(1))
    lax.fori_loop(3, 6, away, 0)
    pl.when(lead)(lambda: twin_half(0))
    lax.fori_loop(6, 9, away, 0)
    pl.when(lead)(lambda: twin_half(1))
    lax.fori_loop(9, 12, away, 0)
    lax.fori_loop(12, STEPS, near, 0)

    v_copy.wait()
    cvec[...] = (vkeep[...].astype(F32) + vrecv[...].astype(F32)).astype(BF16)

    def drain(t, _):
        x_copy(t).wait_send()
        return 0

    lax.fori_loop(0, STEPS, drain, 0)

    def sent(t, _):
        for o in range(4):
            z_copy(t, o).wait_send()
        return 0

    def sent_near(t, _):
        for o in range(1, 4):
            z_copy(t, o).wait_send()
        stay_copy(t).wait()
        return 0

    lax.fori_loop(0, 12, sent, 0)
    lax.fori_loop(12, STEPS, sent_near, 0)
    for p in range(PIECES):
        for test, copy in forwards(p):
            when(test, copy.wait_send)

    def arrived(o, _):
        c = (col + o) % COLS
        for q in range(4):
            pltpu.make_async_remote_copy(
                src_ref=quarter(0, 0), dst_ref=window(c, q), send_sem=zs_sem.at[0],
                recv_sem=zr_sem.at[c * 4 + q], device_id=(row, c), device_id_type=MESH,
            ).wait_recv()
        return 0

    lax.fori_loop(1, COLS, arrived, 0)


def on_device(laplacian, interp, vectors, pairs):
    hbm = pl.BlockSpec(memory_space=pltpu.HBM)
    free = pl.BlockSpec(memory_space=pl.ANY)
    vmem = pl.BlockSpec(memory_space=pltpu.VMEM)
    dma = pltpu.SemaphoreType.DMA
    halves = (KEEP, 4, TILE, WIDE)
    block = (FINE_ROWS * TILE, TILE)
    side = (STRIP, KEEP * TILE)
    shape = jax.ShapeDtypeStruct
    give, keep, mine, vgive, vkeep = pl.pallas_call(
        prepare,
        out_shape=(shape(halves, BF16), shape(halves, F32), shape(block, BF16), shape(side, BF16), shape(side, BF16)),
        in_specs=[pl.BlockSpec(memory_space=pltpu.SMEM), hbm, hbm, hbm],
        out_specs=(free, free, free, vmem, vmem),
        scratch_shapes=[
            pltpu.VMEM((FINE_ROWS, TILE, FINE_COLS * TILE), BF16),
            pltpu.VMEM(block, BF16),
            pltpu.VMEM((STRIP, FINE_ROWS * TILE), BF16),
            pltpu.VMEM(halves, BF16),
            pltpu.VMEM(halves, F32),
            pltpu.VMEM(block, BF16),
            dma((10,)),
            dma((9,)),
        ],
        compiler_params=pltpu.CompilerParams(vmem_limit_bytes=62 * 1024 * 1024),
    )(pairs.T, laplacian, interp, vectors)
    strips, coarse_vectors = pl.pallas_call(
        kernel,
        out_shape=(shape((2, STRIP, COARSE), BF16), shape(side, BF16)),
        in_specs=[free, free, free, vmem, vmem],
        out_specs=(free, vmem),
        scratch_shapes=[
            pltpu.VMEM(halves, F32),
            pltpu.VMEM((FINE_COLS * TILE, TILE), BF16),
            pltpu.VMEM((STEPS, TILE, WIDE), BF16),
            pltpu.VMEM((STEPS, TILE, WIDE), BF16),
            pltpu.VMEM(side, BF16),
            dma((2,)),
            dma((STEPS,)),
            dma((STEPS,)),
            dma((4 * STEPS,)),
            dma((4 * COLS,)),
            dma((5 * PIECES,)),
            dma((2 * PIECES,)),
            dma((2,)),
            pltpu.SemaphoreType.REGULAR,
            pltpu.SemaphoreType.REGULAR,
        ],
        compiler_params=pltpu.CompilerParams(
            collective_id=0, has_side_effects=True, vmem_limit_bytes=62 * 1024 * 1024
        ),
    )(give, keep, mine, vgive, vkeep)
    coarse = (strips[0].astype(F32) + strips[1].astype(F32)).astype(BF16)
    return coarse, coarse_vectors


def solution(mesh):
    placed = (P("row", "col"), P("row", None), P(None, "row"), P())
    return jax.shard_map(
        on_device,
        mesh=mesh,
        in_specs=placed,
        out_specs=(P(("row", "col"), None), P(None, "row")),
        check_vma=False,
    )
```

```python
import jax
import jax.numpy as jnp
from jax import lax
from jax.experimental import pallas as pl
from jax.experimental.pallas import tpu as pltpu
from jax.sharding import PartitionSpec as P

MESH = pl.DeviceIdType.MESH
F32 = jnp.float32
BF16 = jnp.bfloat16

TILE = 128
ROWS = 32
COLS = 16
FINE_ROWS = 8
FINE_COLS = 16
KEEP = 4
STEPS = 16
AHEAD = 2
WIDE = 4 * TILE
STRIP = 32
COARSE = 16384
PIECES = 4
HALF = PIECES // 2
PIECE = FINE_ROWS * TILE // PIECES


def prepare(
    pairs, lap_hbm, interp_hbm, vec_hbm, give_hbm, keep_hbm, block_hbm, vgive, vkeep,
    lap, own, vec, give, keep, block, in_sem, out_sem,
):
    row = lax.axis_index("row")
    col = lax.axis_index("col")
    partner = (row + ROWS // 2) % ROWS
    upper = row // (ROWS // 2)
    right = col // (COLS // 2)
    span = col % (COLS // 2)

    def wanted(k):
        return pairs[upper, KEEP * partner + k] - FINE_ROWS * row

    def kept(k):
        return pairs[upper, KEEP * row + k] - FINE_ROWS * row

    def tile_at(i):
        return pl.ds(pl.multiple_of(i * TILE, TILE), TILE)

    own_in = pltpu.make_async_copy(interp_hbm, own, in_sem.at[8])
    own_in.start()
    members = [wanted(k) for k in range(KEEP)] + [kept(k) for k in range(KEEP)]
    lap_in = []
    for n, i in enumerate(members):
        lap_in.append(pltpu.make_async_copy(lap_hbm.at[tile_at(i)], lap.at[n], in_sem.at[n]))
        lap_in[-1].start()
    vec_in = pltpu.make_async_copy(vec_hbm, vec, in_sem.at[9])
    vec_in.start()
    own_in.wait()

    for u in range(FINE_ROWS):
        d = (u // 4) * 64 + 4 * (row % (ROWS // 2)) + u % 4
        block[u * TILE : (u + 1) * TILE, :] = own[tile_at(pairs[upper, d] - FINE_ROWS * row), :]
    out = [pltpu.make_async_copy(block, block_hbm, out_sem.at[8])]
    out[0].start()

    vec_in.wait()
    for n, i in enumerate(members):
        part = jnp.dot(vec[:, tile_at(i)], own[tile_at(i), :], preferred_element_type=F32).astype(BF16)
        k = n % KEEP
        (vgive if n < KEEP else vkeep)[:, k * TILE : (k + 1) * TILE] = part

    across = [
        tile_at(pairs[right, (q % 2) * 64 + 8 * span + (q // 2) * 4 + v] - FINE_COLS * col)
        for q in range(4)
        for v in range(4)
    ]
    for n, i in enumerate(members):
        lap_in[n].wait()
        k = n % KEEP
        mine = own[tile_at(i), :]
        for q in range(4):
            wide = jnp.concatenate([lap[n, :, across[4 * q + v]] for v in range(4)], axis=1)
            part = lax.dot_general(mine, wide, (((0,), (0,)), ((), ())), preferred_element_type=F32)
            if n < KEEP:
                give[k, q] = part.astype(BF16)
            else:
                keep[k, q] = part
        src, dst = (give, give_hbm) if n < KEEP else (keep, keep_hbm)
        out.append(pltpu.make_async_copy(src.at[k], dst.at[k], out_sem.at[n]))
        out[-1].start()
    for copy in out:
        copy.wait()


def kernel(
    give, keep_hbm, block_hbm, vgive, vkeep, strips, cvec,
    keep, cols, trecv, rsend, vrecv,
    in_sem, xs_sem, xr_sem, zs_sem, zr_sem, ps_sem, pr_sem, v_sem, z_word, y_word,
):
    row = lax.axis_index("row")
    col = lax.axis_index("col")
    x, zlo, core = row // 8, (row // 2) % 4, row % 2
    zhi, y = col // 4, col % 4
    partner = (row + ROWS // 2) % ROWS
    x_up, x_down = (row + 8) % ROWS, (row + 24) % ROWS
    z = zhi * 4 + zlo

    def along(d):
        far = (z + d + 16) % 16
        return x * 8 + far % 4 * 2 + core, far // 4 * 4 + y

    line = [along(d) for d in (1, -1, 2, -2)]
    served = [along(1), along(-1), along(2 - 4 * core)]
    ring = [x_up, x_down, partner]
    twin = row + 1 - 2 * core

    barrier = pltpu.get_barrier_semaphore()

    def greet(r, c):
        pl.semaphore_signal(barrier, inc=1, device_id=(r, c), device_id_type=MESH)

    for r in ring + [twin]:
        greet(r, col)
    for r, c in line:
        greet(r, c)
    z_mates = [(zhi + 1) % 4 * 4 + y, (zhi + 3) % 4 * 4 + y]
    y_mates = [zhi * 4 + (y + o) % 4 for o in range(1, 4)]
    for c in z_mates + y_mates:
        greet(row, c)

    on_row = zlo == y
    dx = (x - zhi + 4) % 4
    column = dx == 0
    aside = jnp.logical_not(column)
    is_source = jnp.logical_and(on_row, column)
    relay = jnp.logical_not(is_source)
    lead = core == 0
    follow = jnp.logical_not(lead)
    mine = pl.ds(pl.multiple_of(core * FINE_ROWS * TILE, FINE_ROWS * TILE), FINE_ROWS * TILE)

    @pl.when(is_source)
    def _():
        copy = pltpu.make_async_copy(block_hbm, cols.at[mine], in_sem.at[1])
        copy.start()
        copy.wait()

    keep_in = pltpu.make_async_copy(keep_hbm, keep, in_sem.at[0])
    keep_in.start()

    pl.semaphore_wait(barrier, len(ring + line) + 1 + len(z_mates + y_mates))

    def place(p):
        return cols.at[pl.ds(pl.multiple_of(core * FINE_ROWS * TILE + p * PIECE, PIECE), PIECE)]

    def piece_copy(p, f, target, sem):
        return pltpu.make_async_remote_copy(
            src_ref=place(p), dst_ref=place(p), send_sem=ps_sem.at[p * 7 + f], recv_sem=pr_sem.at[sem],
            device_id=(target, col), device_id_type=MESH,
        )

    def serves(p):
        out = []
        for f, (r, c) in enumerate(served):
            copy = pltpu.make_async_remote_copy(
                src_ref=block_hbm.at[pl.ds(p * PIECE, PIECE)], dst_ref=place(p), send_sem=ps_sem.at[p * 7 + f],
                recv_sem=pr_sem.at[p], device_id=(r, c), device_id_type=MESH,
            )
            out.append((jnp.logical_and(on_row, c // 4 == x), copy))
        return out

    def forwards(p):
        to_ring = [(column, piece_copy(p, 3 + f, r, p)) for f, r in enumerate(ring)]
        return to_ring + [(None, piece_copy(p, 6, twin, PIECES + p))]

    def when(test, act):
        if test is None:
            act()
        else:
            pl.when(test)(act)

    def pass_on(p):
        for test, copy in forwards(p):
            when(test, copy.start)

    def serve():
        for p in range(PIECES):
            for test, copy in serves(p):
                when(test, copy.start)

    def take(low, high):
        for p in range(low, high):
            pl.when(relay)(piece_copy(p, 0, twin, p).wait_recv)
            pass_on(p)

    def take_all():
        take(0, PIECES)

    def twin_half(n):
        for p in range(n * HALF, (n + 1) * HALF):
            other = cols.at[pl.ds(pl.multiple_of((1 - core) * FINE_ROWS * TILE + p * PIECE, PIECE), PIECE)]
            pltpu.make_async_remote_copy(
                src_ref=other, dst_ref=other, send_sem=ps_sem.at[p * 7 + 6], recv_sem=pr_sem.at[PIECES + p],
                device_id=(twin, col), device_id_type=MESH,
            ).wait_recv()

    def part_of(t):
        far = t < 12
        q = jnp.where(far, t // 3, t - 12)
        k = jnp.where(far, (zhi + 2 - t % 3 + t % 3 // 2 * 3) % 4, zhi)
        return k, q

    def x_copy(t):
        k, q = part_of(t)
        return pltpu.make_async_remote_copy(
            src_ref=give.at[k, q], dst_ref=trecv.at[t], send_sem=xs_sem.at[t], recv_sem=xr_sem.at[t],
            device_id=(partner, col), device_id_type=MESH,
        )

    pl.when(lead)(serve)
    pl.when(aside)(x_copy(0).start)
    for c in z_mates:
        pl.semaphore_signal(z_word, inc=1, device_id=(row, c), device_id_type=MESH)
    pl.when(jnp.logical_and(lead, column))(take_all)
    pl.when(column)(x_copy(0).start)
    pl.semaphore_wait(z_word, 2)
    for c in y_mates:
        pl.semaphore_signal(y_word, inc=1, device_id=(row, c), device_id_type=MESH)
    pl.when(follow)(serve)
    pl.when(jnp.logical_and(lead, aside))(lambda: take(0, HALF))
    pl.when(jnp.logical_and(follow, column))(take_all)
    pl.when(jnp.logical_and(follow, aside))(take_all)
    for t in range(1, AHEAD):
        x_copy(t).start()
    v_copy = pltpu.make_async_remote_copy(
        src_ref=vgive, dst_ref=vrecv, send_sem=v_sem.at[0], recv_sem=v_sem.at[1],
        device_id=(partner, col), device_id_type=MESH,
    )
    v_copy.start()
    keep_in.wait()
    pl.semaphore_wait(y_word, 3)

    def window(c, q):
        start = (q % 2) * (COARSE // 2) + (2 * (c % 8) + q // 2) * WIDE
        return strips.at[c // 8, :, pl.ds(pl.multiple_of(start, WIDE), WIDE)]

    def quarter(t, at):
        return rsend.at[t, pl.ds(pl.multiple_of(at * STRIP, STRIP), STRIP)]

    def z_copy(t, o):
        k, q = part_of(t)
        at = (y + o) % 4
        return pltpu.make_async_remote_copy(
            src_ref=quarter(t, at), dst_ref=window(col, q), send_sem=zs_sem.at[t * 4 + o],
            recv_sem=zr_sem.at[col * 4 + q], device_id=(row, k * 4 + at), device_id_type=MESH,
        )

    def stay_copy(t):
        q = t - 12
        return pltpu.make_async_copy(quarter(t, y), window(col, q), zr_sem.at[col * 4 + q])

    def finish(t):
        @pl.when(t + AHEAD < STEPS)
        def _():
            x_copy(t + AHEAD).start()

        x_copy(t).wait_recv()
        k, q = part_of(t)
        total = (keep[k, q] + trecv[t].astype(F32)).astype(BF16)
        for v in range(4):
            here = slice(v * TILE, (v + 1) * TILE)
            there = pl.ds(pl.multiple_of((q * 4 + v) * TILE, TILE), TILE)
            rsend[t, :, here] = jnp.dot(
                total[:, here], cols[there, :], preferred_element_type=F32
            ).astype(BF16)

    def away(t, _):
        finish(t)
        for o in range(4):
            z_copy(t, o).start()
        return 0

    def near(t, _):
        finish(t)
        for o in range(1, 4):
            z_copy(t, o).start()
        stay_copy(t).start()
        return 0

    pl.when(follow)(lambda: twin_half(0))
    lax.fori_loop(0, 3, away, 0)
    pl.when(jnp.logical_and(lead, aside))(lambda: take(HALF, PIECES))
    pl.when(follow)(lambda: twin_half(1))
    lax.fori_loop(3, 6, away, 0)
    pl.when(lead)(lambda: twin_half(0))
    lax.fori_loop(6, 9, away, 0)
    pl.when(lead)(lambda: twin_half(1))
    lax.fori_loop(9, 12, away, 0)
    lax.fori_loop(12, STEPS, near, 0)

    v_copy.wait()
    cvec[...] = (vkeep[...].astype(F32) + vrecv[...].astype(F32)).astype(BF16)

    def drain(t, _):
        x_copy(t).wait_send()
        return 0

    lax.fori_loop(0, STEPS, drain, 0)

    def sent(t, _):
        for o in range(4):
            z_copy(t, o).wait_send()
        return 0

    def sent_near(t, _):
        for o in range(1, 4):
            z_copy(t, o).wait_send()
        stay_copy(t).wait()
        return 0

    lax.fori_loop(0, 12, sent, 0)
    lax.fori_loop(12, STEPS, sent_near, 0)
    for p in range(PIECES):
        for test, copy in serves(p) + forwards(p):
            when(test, copy.wait_send)

    def arrived(o, _):
        c = (col + o) % COLS
        for q in range(4):
            pltpu.make_async_remote_copy(
                src_ref=quarter(0, 0), dst_ref=window(c, q), send_sem=zs_sem.at[0],
                recv_sem=zr_sem.at[c * 4 + q], device_id=(row, c), device_id_type=MESH,
            ).wait_recv()
        return 0

    lax.fori_loop(1, COLS, arrived, 0)


def on_device(laplacian, interp, vectors, pairs):
    hbm = pl.BlockSpec(memory_space=pltpu.HBM)
    free = pl.BlockSpec(memory_space=pl.ANY)
    vmem = pl.BlockSpec(memory_space=pltpu.VMEM)
    dma = pltpu.SemaphoreType.DMA
    halves = (KEEP, 4, TILE, WIDE)
    block = (FINE_ROWS * TILE, TILE)
    side = (STRIP, KEEP * TILE)
    shape = jax.ShapeDtypeStruct
    give, keep, mine, vgive, vkeep = pl.pallas_call(
        prepare,
        out_shape=(shape(halves, BF16), shape(halves, F32), shape(block, BF16), shape(side, BF16), shape(side, BF16)),
        in_specs=[pl.BlockSpec(memory_space=pltpu.SMEM), hbm, hbm, hbm],
        out_specs=(free, free, free, vmem, vmem),
        scratch_shapes=[
            pltpu.VMEM((FINE_ROWS, TILE, FINE_COLS * TILE), BF16),
            pltpu.VMEM(block, BF16),
            pltpu.VMEM((STRIP, FINE_ROWS * TILE), BF16),
            pltpu.VMEM(halves, BF16),
            pltpu.VMEM(halves, F32),
            pltpu.VMEM(block, BF16),
            dma((10,)),
            dma((9,)),
        ],
        compiler_params=pltpu.CompilerParams(vmem_limit_bytes=62 * 1024 * 1024),
    )(pairs.T, laplacian, interp, vectors)
    strips, coarse_vectors = pl.pallas_call(
        kernel,
        out_shape=(shape((2, STRIP, COARSE), BF16), shape(side, BF16)),
        in_specs=[free, free, free, vmem, vmem],
        out_specs=(free, vmem),
        scratch_shapes=[
            pltpu.VMEM(halves, F32),
            pltpu.VMEM((FINE_COLS * TILE, TILE), BF16),
            pltpu.VMEM((STEPS, TILE, WIDE), BF16),
            pltpu.VMEM((STEPS, TILE, WIDE), BF16),
            pltpu.VMEM(side, BF16),
            dma((2,)),
            dma((STEPS,)),
            dma((STEPS,)),
            dma((4 * STEPS,)),
            dma((4 * COLS,)),
            dma((7 * PIECES,)),
            dma((2 * PIECES,)),
            dma((2,)),
            pltpu.SemaphoreType.REGULAR,
            pltpu.SemaphoreType.REGULAR,
        ],
        compiler_params=pltpu.CompilerParams(
            collective_id=0, has_side_effects=True, vmem_limit_bytes=62 * 1024 * 1024
        ),
    )(give, keep, mine, vgive, vkeep)
    coarse = (strips[0].astype(F32) + strips[1].astype(F32)).astype(BF16)
    return coarse, coarse_vectors


def solution(mesh):
    placed = (P("row", "col"), P("row", None), P(None, "row"), P())
    return jax.shard_map(
        on_device,
        mesh=mesh,
        in_specs=placed,
        out_specs=(P(("row", "col"), None), P(None, "row")),
        check_vma=False,
    )
```

```python
import jax
import jax.numpy as jnp
from jax import lax
from jax.experimental import pallas as pl
from jax.experimental.pallas import tpu as pltpu
from jax.sharding import PartitionSpec as P

MESH = pl.DeviceIdType.MESH
F32 = jnp.float32
BF16 = jnp.bfloat16

TILE = 128
ROWS = 32
COLS = 16
FINE_ROWS = 8
FINE_COLS = 16
KEEP = 4
STEPS = 16
AHEAD = 2
WIDE = 4 * TILE
STRIP = 32
COARSE = 16384
PIECES = 8
HALF = PIECES // 2
PIECE = FINE_ROWS * TILE // PIECES


def prepare(
    pairs, lap_hbm, interp_hbm, vec_hbm, give_hbm, keep_hbm, block_hbm, vgive, vkeep,
    lap, own, vec, give, keep, block, in_sem, out_sem,
):
    row = lax.axis_index("row")
    col = lax.axis_index("col")
    partner = (row + ROWS // 2) % ROWS
    upper = row // (ROWS // 2)
    right = col // (COLS // 2)
    span = col % (COLS // 2)

    def wanted(k):
        return pairs[upper, KEEP * partner + k] - FINE_ROWS * row

    def kept(k):
        return pairs[upper, KEEP * row + k] - FINE_ROWS * row

    def tile_at(i):
        return pl.ds(pl.multiple_of(i * TILE, TILE), TILE)

    own_in = pltpu.make_async_copy(interp_hbm, own, in_sem.at[8])
    own_in.start()
    members = [wanted(k) for k in range(KEEP)] + [kept(k) for k in range(KEEP)]
    lap_in = []
    for n, i in enumerate(members):
        lap_in.append(pltpu.make_async_copy(lap_hbm.at[tile_at(i)], lap.at[n], in_sem.at[n]))
        lap_in[-1].start()
    vec_in = pltpu.make_async_copy(vec_hbm, vec, in_sem.at[9])
    vec_in.start()
    own_in.wait()

    for u in range(FINE_ROWS):
        d = (u // 4) * 64 + 4 * (row % (ROWS // 2)) + u % 4
        block[u * TILE : (u + 1) * TILE, :] = own[tile_at(pairs[upper, d] - FINE_ROWS * row), :]
    out = [pltpu.make_async_copy(block, block_hbm, out_sem.at[8])]
    out[0].start()

    vec_in.wait()
    for n, i in enumerate(members):
        part = jnp.dot(vec[:, tile_at(i)], own[tile_at(i), :], preferred_element_type=F32).astype(BF16)
        k = n % KEEP
        (vgive if n < KEEP else vkeep)[:, k * TILE : (k + 1) * TILE] = part

    across = [
        tile_at(pairs[right, (q % 2) * 64 + 8 * span + (q // 2) * 4 + v] - FINE_COLS * col)
        for q in range(4)
        for v in range(4)
    ]
    for n, i in enumerate(members):
        lap_in[n].wait()
        k = n % KEEP
        mine = own[tile_at(i), :]
        for q in range(4):
            wide = jnp.concatenate([lap[n, :, across[4 * q + v]] for v in range(4)], axis=1)
            part = lax.dot_general(mine, wide, (((0,), (0,)), ((), ())), preferred_element_type=F32)
            if n < KEEP:
                give[k, q] = part.astype(BF16)
            else:
                keep[k, q] = part
        src, dst = (give, give_hbm) if n < KEEP else (keep, keep_hbm)
        out.append(pltpu.make_async_copy(src.at[k], dst.at[k], out_sem.at[n]))
        out[-1].start()
    for copy in out:
        copy.wait()


def kernel(
    give, keep_hbm, block_hbm, vgive, vkeep, strips, cvec,
    keep, cols, trecv, rsend, vrecv,
    in_sem, xs_sem, xr_sem, zs_sem, zr_sem, ps_sem, pr_sem, v_sem, z_word, y_word,
):
    row = lax.axis_index("row")
    col = lax.axis_index("col")
    x, zlo, core = row // 8, (row // 2) % 4, row % 2
    zhi, y = col // 4, col % 4
    partner = (row + ROWS // 2) % ROWS
    x_up, x_down = (row + 8) % ROWS, (row + 24) % ROWS
    z = zhi * 4 + zlo

    def along(d):
        far = (z + d + 16) % 16
        return x * 8 + far % 4 * 2 + core, far // 4 * 4 + y

    line = [along(d) for d in (1, -1, 2, -2)]
    served = [along(1), along(-1), along(2 - 4 * core)]
    ring = [x_up, x_down, partner]
    twin = row + 1 - 2 * core

    barrier = pltpu.get_barrier_semaphore()

    def greet(r, c):
        pl.semaphore_signal(barrier, inc=1, device_id=(r, c), device_id_type=MESH)

    for r in ring + [twin]:
        greet(r, col)
    for r, c in line:
        greet(r, c)
    z_mates = [(zhi + 1) % 4 * 4 + y, (zhi + 3) % 4 * 4 + y]
    y_mates = [zhi * 4 + (y + o) % 4 for o in range(1, 4)]
    for c in z_mates + y_mates:
        greet(row, c)

    on_row = zlo == y
    dx = (x - zhi + 4) % 4
    column = dx == 0
    aside = jnp.logical_not(column)
    is_source = jnp.logical_and(on_row, column)
    relay = jnp.logical_not(is_source)
    lead = core == 0
    follow = jnp.logical_not(lead)
    mine = pl.ds(pl.multiple_of(core * FINE_ROWS * TILE, FINE_ROWS * TILE), FINE_ROWS * TILE)

    @pl.when(is_source)
    def _():
        copy = pltpu.make_async_copy(block_hbm, cols.at[mine], in_sem.at[1])
        copy.start()
        copy.wait()

    keep_in = pltpu.make_async_copy(keep_hbm, keep, in_sem.at[0])
    keep_in.start()

    pl.semaphore_wait(barrier, len(ring + line) + 1 + len(z_mates + y_mates))

    def place(p):
        return cols.at[pl.ds(pl.multiple_of(core * FINE_ROWS * TILE + p * PIECE, PIECE), PIECE)]

    def piece_copy(p, f, target, sem):
        return pltpu.make_async_remote_copy(
            src_ref=place(p), dst_ref=place(p), send_sem=ps_sem.at[p * 7 + f], recv_sem=pr_sem.at[sem],
            device_id=(target, col), device_id_type=MESH,
        )

    def serves(p):
        out = []
        for f, (r, c) in enumerate(served):
            copy = pltpu.make_async_remote_copy(
                src_ref=block_hbm.at[pl.ds(p * PIECE, PIECE)], dst_ref=place(p), send_sem=ps_sem.at[p * 7 + f],
                recv_sem=pr_sem.at[p], device_id=(r, c), device_id_type=MESH,
            )
            out.append((jnp.logical_and(on_row, c // 4 == x), copy))
        return out

    def forwards(p):
        to_ring = [(column, piece_copy(p, 3 + f, r, p)) for f, r in enumerate(ring)]
        return to_ring + [(None, piece_copy(p, 6, twin, PIECES + p))]

    def when(test, act):
        if test is None:
            act()
        else:
            pl.when(test)(act)

    def pass_on(p):
        for test, copy in forwards(p):
            when(test, copy.start)

    def serve():
        for p in range(PIECES):
            for test, copy in serves(p):
                when(test, copy.start)

    def take(low, high):
        for p in range(low, high):
            pl.when(relay)(piece_copy(p, 0, twin, p).wait_recv)
            pass_on(p)

    def take_all():
        take(0, PIECES)

    def twin_half(n):
        for p in range(n * HALF, (n + 1) * HALF):
            other = cols.at[pl.ds(pl.multiple_of((1 - core) * FINE_ROWS * TILE + p * PIECE, PIECE), PIECE)]
            pltpu.make_async_remote_copy(
                src_ref=other, dst_ref=other, send_sem=ps_sem.at[p * 7 + 6], recv_sem=pr_sem.at[PIECES + p],
                device_id=(twin, col), device_id_type=MESH,
            ).wait_recv()

    def part_of(t):
        far = t < 12
        q = jnp.where(far, t // 3, t - 12)
        k = jnp.where(far, (zhi + 2 - t % 3 + t % 3 // 2 * 3) % 4, zhi)
        return k, q

    def x_copy(t):
        k, q = part_of(t)
        return pltpu.make_async_remote_copy(
            src_ref=give.at[k, q], dst_ref=trecv.at[t], send_sem=xs_sem.at[t], recv_sem=xr_sem.at[t],
            device_id=(partner, col), device_id_type=MESH,
        )

    pl.when(lead)(serve)
    pl.when(aside)(x_copy(0).start)
    for c in z_mates:
        pl.semaphore_signal(z_word, inc=1, device_id=(row, c), device_id_type=MESH)
    pl.when(jnp.logical_and(lead, column))(take_all)
    pl.when(column)(x_copy(0).start)
    pl.semaphore_wait(z_word, 2)
    for c in y_mates:
        pl.semaphore_signal(y_word, inc=1, device_id=(row, c), device_id_type=MESH)
    pl.when(follow)(serve)
    pl.when(jnp.logical_and(lead, aside))(lambda: take(0, HALF))
    pl.when(jnp.logical_and(follow, column))(take_all)
    pl.when(jnp.logical_and(follow, aside))(take_all)
    for t in range(1, AHEAD):
        x_copy(t).start()
    v_copy = pltpu.make_async_remote_copy(
        src_ref=vgive, dst_ref=vrecv, send_sem=v_sem.at[0], recv_sem=v_sem.at[1],
        device_id=(partner, col), device_id_type=MESH,
    )
    v_copy.start()
    keep_in.wait()
    pl.semaphore_wait(y_word, 3)

    def window(c, q):
        start = (q % 2) * (COARSE // 2) + (2 * (c % 8) + q // 2) * WIDE
        return strips.at[c // 8, :, pl.ds(pl.multiple_of(start, WIDE), WIDE)]

    def quarter(t, at):
        return rsend.at[t, pl.ds(pl.multiple_of(at * STRIP, STRIP), STRIP)]

    def z_copy(t, o):
        k, q = part_of(t)
        at = (y + o) % 4
        return pltpu.make_async_remote_copy(
            src_ref=quarter(t, at), dst_ref=window(col, q), send_sem=zs_sem.at[t * 4 + o],
            recv_sem=zr_sem.at[col * 4 + q], device_id=(row, k * 4 + at), device_id_type=MESH,
        )

    def stay_copy(t):
        q = t - 12
        return pltpu.make_async_copy(quarter(t, y), window(col, q), zr_sem.at[col * 4 + q])

    def finish(t):
        @pl.when(t + AHEAD < STEPS)
        def _():
            x_copy(t + AHEAD).start()

        x_copy(t).wait_recv()
        k, q = part_of(t)
        total = (keep[k, q] + trecv[t].astype(F32)).astype(BF16)
        for v in range(4):
            here = slice(v * TILE, (v + 1) * TILE)
            there = pl.ds(pl.multiple_of((q * 4 + v) * TILE, TILE), TILE)
            rsend[t, :, here] = jnp.dot(
                total[:, here], cols[there, :], preferred_element_type=F32
            ).astype(BF16)

    def away(t, _):
        finish(t)
        for o in range(4):
            z_copy(t, o).start()
        return 0

    def near(t, _):
        finish(t)
        for o in range(1, 4):
            z_copy(t, o).start()
        stay_copy(t).start()
        return 0

    pl.when(follow)(lambda: twin_half(0))
    lax.fori_loop(0, 3, away, 0)
    pl.when(jnp.logical_and(lead, aside))(lambda: take(HALF, PIECES))
    pl.when(follow)(lambda: twin_half(1))
    lax.fori_loop(3, 6, away, 0)
    pl.when(lead)(lambda: twin_half(0))
    lax.fori_loop(6, 9, away, 0)
    pl.when(lead)(lambda: twin_half(1))
    lax.fori_loop(9, 12, away, 0)
    lax.fori_loop(12, STEPS, near, 0)

    v_copy.wait()
    cvec[...] = (vkeep[...].astype(F32) + vrecv[...].astype(F32)).astype(BF16)

    def drain(t, _):
        x_copy(t).wait_send()
        return 0

    lax.fori_loop(0, STEPS, drain, 0)

    def sent(t, _):
        for o in range(4):
            z_copy(t, o).wait_send()
        return 0

    def sent_near(t, _):
        for o in range(1, 4):
            z_copy(t, o).wait_send()
        stay_copy(t).wait()
        return 0

    lax.fori_loop(0, 12, sent, 0)
    lax.fori_loop(12, STEPS, sent_near, 0)
    for p in range(PIECES):
        for test, copy in serves(p) + forwards(p):
            when(test, copy.wait_send)

    def arrived(o, _):
        c = (col + o) % COLS
        for q in range(4):
            pltpu.make_async_remote_copy(
                src_ref=quarter(0, 0), dst_ref=window(c, q), send_sem=zs_sem.at[0],
                recv_sem=zr_sem.at[c * 4 + q], device_id=(row, c), device_id_type=MESH,
            ).wait_recv()
        return 0

    lax.fori_loop(1, COLS, arrived, 0)


def on_device(laplacian, interp, vectors, pairs):
    hbm = pl.BlockSpec(memory_space=pltpu.HBM)
    free = pl.BlockSpec(memory_space=pl.ANY)
    vmem = pl.BlockSpec(memory_space=pltpu.VMEM)
    dma = pltpu.SemaphoreType.DMA
    halves = (KEEP, 4, TILE, WIDE)
    block = (FINE_ROWS * TILE, TILE)
    side = (STRIP, KEEP * TILE)
    shape = jax.ShapeDtypeStruct
    give, keep, mine, vgive, vkeep = pl.pallas_call(
        prepare,
        out_shape=(shape(halves, BF16), shape(halves, F32), shape(block, BF16), shape(side, BF16), shape(side, BF16)),
        in_specs=[pl.BlockSpec(memory_space=pltpu.SMEM), hbm, hbm, hbm],
        out_specs=(free, free, free, vmem, vmem),
        scratch_shapes=[
            pltpu.VMEM((FINE_ROWS, TILE, FINE_COLS * TILE), BF16),
            pltpu.VMEM(block, BF16),
            pltpu.VMEM((STRIP, FINE_ROWS * TILE), BF16),
            pltpu.VMEM(halves, BF16),
            pltpu.VMEM(halves, F32),
            pltpu.VMEM(block, BF16),
            dma((10,)),
            dma((9,)),
        ],
        compiler_params=pltpu.CompilerParams(vmem_limit_bytes=62 * 1024 * 1024),
    )(pairs.T, laplacian, interp, vectors)
    strips, coarse_vectors = pl.pallas_call(
        kernel,
        out_shape=(shape((2, STRIP, COARSE), BF16), shape(side, BF16)),
        in_specs=[free, free, free, vmem, vmem],
        out_specs=(free, vmem),
        scratch_shapes=[
            pltpu.VMEM(halves, F32),
            pltpu.VMEM((FINE_COLS * TILE, TILE), BF16),
            pltpu.VMEM((STEPS, TILE, WIDE), BF16),
            pltpu.VMEM((STEPS, TILE, WIDE), BF16),
            pltpu.VMEM(side, BF16),
            dma((2,)),
            dma((STEPS,)),
            dma((STEPS,)),
            dma((4 * STEPS,)),
            dma((4 * COLS,)),
            dma((7 * PIECES,)),
            dma((2 * PIECES,)),
            dma((2,)),
            pltpu.SemaphoreType.REGULAR,
            pltpu.SemaphoreType.REGULAR,
        ],
        compiler_params=pltpu.CompilerParams(
            collective_id=0, has_side_effects=True, vmem_limit_bytes=62 * 1024 * 1024
        ),
    )(give, keep, mine, vgive, vkeep)
    coarse = (strips[0].astype(F32) + strips[1].astype(F32)).astype(BF16)
    return coarse, coarse_vectors


def solution(mesh):
    placed = (P("row", "col"), P("row", None), P(None, "row"), P())
    return jax.shard_map(
        on_device,
        mesh=mesh,
        in_specs=placed,
        out_specs=(P(("row", "col"), None), P(None, "row")),
        check_vma=False,
    )
```
